128 devices in a mesh: seq: 4 (over y), expert: 32 (over z, x, core).
Axes of the slice: x: 4, y: 4, z: 4, core: 2. Of those that a mesh axis runs over, the one named last changes fastest.
Arguments:
- frames: bfloat16 [16384, 1536], P(('seq', 'expert')), may hold values from -6 to 6
- expert_ids: int32 [16384, 2], P(('seq', 'expert')), may hold values from 0 to 31, all different within a row; in each aligned block of 128 rows (0 to 127, 128 to 255, ...) at most 16 rows name the same one
- gate_weights: float32 [16384, 2], P(('seq', 'expert')), may hold values from 0.2 to 1
- up_weight: bfloat16 [32, 1536, 2048], P('expert'), may hold values from -0.15625 to 0.15625
- down_weight: bfloat16 [32, 2048, 1536], P('expert'), may hold values from -0.125 to 0.125
- smooth_taps: float32 [9, 1536], replicated, may hold values from -0.1 to 0.4
- head_weight: bfloat16 [1536, 527], replicated, may hold values from -0.15625 to 0.15625
- logit_grad: bfloat16 [16384, 527], P(('seq', 'expert')), may hold values from -6 to 6
Outputs:
- logits: bfloat16 [16384, 527], P(('seq', 'expert'))
- frame_grad: bfloat16 [16384, 1536], P(('seq', 'expert'))
- gate_grad: float32 [16384, 2], P(('seq', 'expert'))
The draws below stay inside these ranges and needn't reach their ends.
Inputs may be any that keep to these rules, and one draw needn't show every extreme that they name: `expert_ids`: the two experts of a frame differ. Among the 256 choices of each aligned block of 128 frames (one device's frames) no expert is named more than 16 times, and in some block some expert is named exactly 16 times.
All inputs are finite; a program needn't handle non-finite values.
Results may differ from the reference program's by a relative error of at most 0.0065.
Values may be sent and summed in bfloat16 or wider, within the bound.
No kernel may reach another device: no remote copies, remote signals or barrier semaphores. Data moves between devices by JAX's collectives and lax.ppermute only.
A program may use at most 128 MiB of HBM per device.

```python
import math
import jax
import jax.numpy as jnp
import numpy as np
from jax import lax

D = 1536
FF = 2048
CLASSES = 527
KW = 9
FR_DEV = 128
EXPERTS = 32
CAP = 16
FRAMES = 16384


def levels(rng, dims, pieces, low, high):
    gain, own = 1.0, jax.random.fold_in(rng, 6)
    for dim, blocks in pieces:
        steps = jnp.exp(jax.random.uniform(jax.random.fold_in(own, dim), (blocks,), jnp.float32, low / len(pieces), high / len(pieces)))
        gain = gain * jnp.repeat(steps, dims[dim] // blocks).reshape([-1 if axis == dim else 1 for axis in range(len(dims))])
    return gain


def shared_out(rng, own, number, rows, number_of, top, reach, slope):
    ranking = jax.random.permutation(rng, number_of)
    packed, usual = portions_of(number_of, rows * top, reach, slope, True), portions_of(number_of, rows * top, reach, slope, False)
    places = jnp.arange(number_of)

    def named(lengths, offset_by):
        used = int((lengths > 0).sum())
        fixed = max(1, used // 4)
        moved = fixed + (places - fixed + offset_by * (used - fixed)) % max(1, number_of - fixed)
        return jnp.zeros((number_of,), jnp.int32).at[ranking[jnp.where(places < fixed, places, moved)]].set(jnp.asarray(lengths, jnp.int32))

    lengths = jnp.where(number % 4 == 0, named(packed, number // 4), named(usual, number - number // 4 - 1))
    mixed = jax.random.permutation(jax.random.fold_in(own, 3), number_of)
    source_of, sink = mixed[0:number_of // 2 * 2:2], mixed[1:number_of // 2 * 2:2]
    room = jnp.minimum(lengths[source_of] - 1, reach - lengths[sink]) // 2
    room = jnp.where((source_of == ranking[0]) | (sink == ranking[0]) | (lengths[sink] == 0), 0, jnp.maximum(room, 0))
    moved = jax.random.randint(jax.random.fold_in(own, 4), (number_of // 2,), 0, 1 << 20) % (room + 1)
    lengths = lengths.at[source_of].add(-moved).at[sink].add(moved)
    labels = jnp.searchsorted(jnp.cumsum(lengths), jnp.arange(rows * top), side="right").astype(jnp.int32)
    listing = labels.reshape(top, rows).T
    listing = listing[jax.random.permutation(jax.random.fold_in(own, 1), rows)]
    offset_by = jax.random.randint(jax.random.fold_in(own, 2), (rows, 1), 0, top)
    return jnp.take_along_axis(listing, (jnp.arange(top)[None, :] + offset_by) % top, axis=1)


def portions_of(number_of, total, most, lean, full):
    loads = [(1 << 20) // math.isqrt(standing ** lean) + 1 for standing in range(1, number_of + 1)]
    largest = most if full else min(most, max(-(-total // number_of), total * loads[0] // sum(loads)))
    least = 1 if total - largest >= number_of - 1 else 0
    given, rest = [largest] + [least] * (number_of - 1), total - largest - least * (number_of - 1)
    while rest > 0:
        free = [i for i in range(1, number_of) if given[i] < largest] or [i for i in range(1, number_of) if given[i] < most]
        pool, left = sum([loads[i] for i in free]), rest
        for i in free:
            more = min(most - given[i], max(1, left * loads[i] // pool), rest)
            given[i] = given[i] + more
            rest = rest - more
    return np.array(given)


def noise(rng, shape, scale, most, shards=(), held_as=jnp.bfloat16):
    level = levels(rng, shape, shards, -0.22, 0.18) if shards else 1.0
    entries = jax.random.normal(rng, shape, jnp.float32) * scale * level
    return jnp.minimum(jnp.maximum(entries, -most), most).astype(held_as)


def setup_inputs(seed: int = 0) -> dict:
    keys = jax.random.split(jax.random.key(seed), 9)
    frames = noise(keys[0], (FRAMES, D), 1.0, 6.0, ((0, 128),))
    expert_ids_keys = jax.random.split(jax.random.fold_in(keys[1], 1), FRAMES // FR_DEV)
    expert_ids_turns = jax.random.permutation(jax.random.fold_in(keys[1], 3), FRAMES // FR_DEV)
    expert_ids = jax.vmap(lambda own, number: shared_out(jax.random.fold_in(keys[1], 2), own, number, FR_DEV, EXPERTS, 2, CAP, 2))(expert_ids_keys, expert_ids_turns).reshape((FRAMES, 2))
    gate_weights = jnp.clip(0.2 + 0.8 * jax.random.uniform(keys[2], (FRAMES, 2), jnp.float32) ** levels(keys[2], (FRAMES, 2), ((0, 128),), -0.2, 0.2), 0.2, 1.0)
    up_weight = noise(keys[3], (EXPERTS, D, FF), D ** -0.5, 0.15625, ((0, 32),))
    down_weight = noise(keys[4], (EXPERTS, FF, D), FF ** -0.5, 0.125, ((0, 32),))
    smooth_taps = jnp.clip(jax.random.uniform(keys[5], (KW, D), jnp.float32, -0.1, 0.4), -0.1, 0.4)
    head_weight = noise(keys[6], (D, CLASSES), D ** -0.5, 0.15625)
    logit_grad = noise(keys[7], (FRAMES, CLASSES), 1.0, 6.0, ((0, 128),))
    return {"frames": frames, "expert_ids": expert_ids, "gate_weights": gate_weights, "up_weight": up_weight, "down_weight": down_weight, "smooth_taps": smooth_taps, "head_weight": head_weight, "logit_grad": logit_grad}


slope_coef = 0.7978845608028654
cubic_coef = 0.044715


def gelu_value(inputs):
    return 0.5 * inputs * (1.0 + jnp.tanh(slope_coef * (inputs + cubic_coef * inputs * inputs * inputs)))


def gelu_slope(inputs):
    inner = jnp.tanh(slope_coef * (inputs + cubic_coef * inputs * inputs * inputs))
    return 0.5 * (1.0 + inner) + 0.5 * inputs * (1.0 - inner * inner) * slope_coef * (1.0 + 3.0 * cubic_coef * inputs * inputs)


def taps_forward(padded, smooth_taps, count):
    summed = jnp.zeros((count, padded.shape[1]), jnp.float32)
    for offset in range(smooth_taps.shape[0]):
        summed = summed + smooth_taps[offset] * padded[offset:offset + count]
    return summed


def taps_backward(padded, smooth_taps, count):
    last_tap = smooth_taps.shape[0] - 1
    summed = jnp.zeros((count, padded.shape[1]), jnp.float32)
    for offset in range(smooth_taps.shape[0]):
        summed = summed + smooth_taps[offset] * padded[last_tap - offset:last_tap - offset + count]
    return summed


def expert_math(slots_x, slots_g, up_one, down_one):
    pre = jnp.dot(slots_x, up_one, preferred_element_type=jnp.float32)
    hidden = gelu_value(pre).astype(jnp.bfloat16)
    outputs = jnp.dot(hidden, down_one, preferred_element_type=jnp.float32).astype(jnp.bfloat16)
    back_hidden = jnp.dot(slots_g, down_one.T, preferred_element_type=jnp.float32)
    pre_grad = (back_hidden * gelu_slope(pre)).astype(jnp.bfloat16)
    parts = jnp.dot(pre_grad, up_one.T, preferred_element_type=jnp.float32).astype(jnp.bfloat16)
    return outputs, parts


def reference(frames, expert_ids, gate_weights, up_weight, down_weight, smooth_taps, head_weight, logit_grad):
    margin = (KW - 1) // 2
    rows_all = FRAMES // FR_DEV * CAP
    flat_ids = expert_ids.reshape(-1)
    smooth_grad = jnp.dot(logit_grad, head_weight.T, preferred_element_type=jnp.float32).astype(jnp.bfloat16)
    smooth_grad = lax.optimization_barrier(smooth_grad)
    grad_padded = jnp.pad(smooth_grad.astype(jnp.float32), ((margin, margin), (0, 0)))
    mixed_grad = taps_backward(grad_padded, smooth_taps, FRAMES).astype(jnp.bfloat16)
    mixed_grad = lax.optimization_barrier(mixed_grad)
    repeated = jnp.repeat(frames, 2, axis=0)
    grad_repeated = jnp.repeat(mixed_grad, 2, axis=0)

    def per_expert(carry, expert):
        outputs, parts = carry
        chosen = flat_ids == expert
        position = jnp.cumsum(chosen.astype(jnp.int32)) - 1
        target = jnp.where(chosen, position, rows_all).astype(jnp.int32)
        slots_x = jnp.zeros((rows_all + 1, D), jnp.bfloat16).at[target].set(repeated)[:rows_all]
        slots_g = jnp.zeros((rows_all + 1, D), jnp.bfloat16).at[target].set(grad_repeated)[:rows_all]
        new_out, new_parts = expert_math(slots_x, slots_g, up_weight[expert], down_weight[expert])
        back_index = jnp.minimum(target, rows_all - 1).astype(jnp.int32)
        outputs = jnp.where(chosen[:, None], new_out[back_index], outputs)
        parts = jnp.where(chosen[:, None], new_parts[back_index], parts)
        return (outputs, parts), None

    empty = jnp.zeros((2 * FRAMES, D), jnp.bfloat16)
    (outputs, parts), unused = lax.scan(per_expert, (empty, empty), jnp.arange(EXPERTS, dtype=jnp.int32))
    outputs = outputs.reshape(FRAMES, 2, D).astype(jnp.float32)
    parts = parts.reshape(FRAMES, 2, D).astype(jnp.float32)
    first_gate = gate_weights[:, 0:1]
    second_gate = gate_weights[:, 1:2]
    mixed = (frames.astype(jnp.float32) + first_gate * outputs[:, 0] + second_gate * outputs[:, 1]).astype(jnp.bfloat16)
    mixed = lax.optimization_barrier(mixed)
    mixed_padded = jnp.pad(mixed.astype(jnp.float32), ((margin, margin), (0, 0)))
    smooth = taps_forward(mixed_padded, smooth_taps, FRAMES).astype(jnp.bfloat16)
    logits = jnp.dot(smooth, head_weight, preferred_element_type=jnp.float32).astype(jnp.bfloat16)
    grad_f32 = mixed_grad.astype(jnp.float32)
    frame_grad = (grad_f32 + first_gate * parts[:, 0] + second_gate * parts[:, 1]).astype(jnp.bfloat16)
    gate_grad = jnp.sum(outputs * grad_f32[:, None, :], axis=2)
    return logits, frame_grad, gate_grad
```

```python
import functools

import jax
import jax.numpy as jnp
from jax import lax
from jax.experimental import pallas as pl
from jax.experimental.pallas import tpu as pltpu
from jax.sharding import PartitionSpec as P

slope_coef = 0.7978845608028654
cubic_coef = 0.044715
bf16 = jnp.bfloat16
f32 = jnp.float32
i32 = jnp.int32


def gelu_value(inputs):
    return (
        0.5
        * inputs
        * (1.0 + jnp.tanh(slope_coef * (inputs + cubic_coef * inputs * inputs * inputs)))
    )


def gelu_slope(inputs):
    inner = jnp.tanh(slope_coef * (inputs + cubic_coef * inputs * inputs * inputs))
    return 0.5 * (1.0 + inner) + 0.5 * inputs * (1.0 - inner * inner) * slope_coef * (
        1.0 + 3.0 * cubic_coef * inputs * inputs
    )


def cost(flops, moved):
    return pl.CostEstimate(flops=flops, bytes_accessed=moved, transcendentals=0)


def whole(shape):
    return pl.BlockSpec(shape, lambda j: (0,) * len(shape))


def cols(rows, tile):
    return pl.BlockSpec((rows, tile), lambda j: (0, j))


def iota(shape, dim):
    return lax.broadcasted_iota(i32, shape, dim)


def to_column(row):
    n = row.shape[1]
    diagonal = iota((n, n), 0) == iota((n, n), 1)
    return jnp.sum(jnp.where(diagonal, row, jnp.zeros_like(row)), axis=1, keepdims=True)


def to_row(column):
    n = column.shape[0]
    diagonal = iota((n, n), 0) == iota((n, n), 1)
    return jnp.sum(jnp.where(diagonal, column, jnp.zeros_like(column)), axis=0, keepdims=True)


def send_mask(target, slots):
    rows = iota((slots, target.shape[1]), 0)
    hit = (rows == target[0:1, :]) | (rows == target[1:2, :])
    return jnp.where(hit, 1.0, 0.0).astype(bf16)


def pick_mask(target_row, slots):
    column = to_column(target_row)
    return jnp.where(iota((column.shape[0], slots), 1) == column, 1.0, 0.0).astype(bf16)


def fill_padded(padded, low, block, high):
    rows = block.shape[0]
    margin = low.shape[0]
    padded[8 - margin : 8, :] = low.astype(f32)
    padded[8 : 8 + rows, :] = block.astype(f32)
    padded[8 + rows : 8 + rows + margin, :] = high.astype(f32)


def dispatch_kernel(owners, capacity, ids_ref, frames_ref, send_ref, target_ref, mask_ref):
    slots = owners * capacity
    count = ids_ref.shape[1]

    @pl.when(pl.program_id(0) == 0)
    def _():
        ids = ids_ref[...]
        first, second = ids[0:1, :], ids[1:2, :]
        experts = iota((owners, count), 0)
        first_hot = jnp.where(experts == first, 1.0, 0.0)
        second_hot = jnp.where(experts == second, 1.0, 0.0)
        before = jnp.where(iota((count, count), 0) < iota((count, count), 1), 1.0, 0.0).astype(bf16)
        first_seen = jnp.dot(first_hot.astype(bf16), before, preferred_element_type=f32)
        second_seen = jnp.dot(second_hot.astype(bf16), before, preferred_element_type=f32)
        second_seen = second_seen + jnp.sum(first_hot, axis=1, keepdims=True)
        first_rank = jnp.sum(first_seen * first_hot, axis=0, keepdims=True).astype(i32)
        second_rank = jnp.sum(second_seen * second_hot, axis=0, keepdims=True).astype(i32)
        target = jnp.concatenate(
            [first * capacity + first_rank, second * capacity + second_rank], axis=0
        )
        target_ref[...] = target
        mask_ref[...] = send_mask(target, slots)

    send_ref[...] = jnp.dot(
        mask_ref[...], frames_ref[...], preferred_element_type=f32
    ).astype(bf16)


def dispatch(ids, frames, owners, capacity, tile=512):
    rows, width = frames.shape
    slots = owners * capacity

    return pl.pallas_call(
        functools.partial(dispatch_kernel, owners, capacity),
        grid=(width // tile,),
        out_shape=(
            jax.ShapeDtypeStruct((slots, width), bf16),
            jax.ShapeDtypeStruct((2, rows), i32),
        ),
        in_specs=[whole((2, rows)), cols(rows, tile)],
        out_specs=(cols(slots, tile), whole((2, rows))),
        scratch_shapes=[pltpu.VMEM((slots, rows), bf16)],
        cost_estimate=cost(2 * slots * rows * width, 2 * (slots + rows) * width),
        name="dispatch",
    )(ids, frames)


def grad_kernel(target_ref, low_ref, block_ref, high_ref, taps_ref, grad_ref, send_ref, mask_ref, padded):
    rows = block_ref.shape[0]
    taps = taps_ref.shape[0]

    @pl.when(pl.program_id(0) == 0)
    def _():
        mask_ref[...] = send_mask(target_ref[...], mask_ref.shape[0])

    fill_padded(padded, low_ref[...], block_ref[...], high_ref[...])
    summed = jnp.zeros(block_ref.shape, f32)
    for offset in range(taps):
        start = 8 - taps // 2 + taps - 1 - offset
        summed = summed + taps_ref[offset : offset + 1, :] * padded[start : start + rows, :]
    grad = summed.astype(bf16)
    grad_ref[...] = grad
    send_ref[...] = jnp.dot(mask_ref[...], grad, preferred_element_type=f32).astype(bf16)


def grad_dispatch(target, low, block, high, taps, slots, tile=512):
    rows, width = block.shape
    margin = low.shape[0]
    return pl.pallas_call(
        grad_kernel,
        grid=(width // tile,),
        out_shape=(
            jax.ShapeDtypeStruct((rows, width), bf16),
            jax.ShapeDtypeStruct((slots, width), bf16),
        ),
        in_specs=[
            whole((2, rows)),
            cols(margin, tile),
            cols(rows, tile),
            cols(margin, tile),
            cols(taps.shape[0], tile),
        ],
        out_specs=(cols(rows, tile), cols(slots, tile)),
        scratch_shapes=[pltpu.VMEM((slots, rows), bf16), pltpu.VMEM((rows + 16, tile), f32)],
        cost_estimate=cost(2 * slots * rows * width, 2 * (slots + 2 * rows) * width),
        name="grad_dispatch",
    )(target, low, block, high, taps)


def mix_kernel(
    target_ref, gates_ref, slots_ref, frames_ref, grad_ref, mixed_ref, gate_grad_ref,
    first_mask, second_mask, gate_columns, sums,
):
    step = pl.program_id(0)

    @pl.when(step == 0)
    def _():
        target = target_ref[...]
        gates = gates_ref[...]
        first_mask[...] = pick_mask(target[0:1, :], first_mask.shape[1])
        second_mask[...] = pick_mask(target[1:2, :], second_mask.shape[1])
        gate_columns[:, 0:1] = to_column(gates[0:1, :])
        gate_columns[:, 1:2] = to_column(gates[1:2, :])
        sums[...] = jnp.zeros_like(sums)

    slots = slots_ref[...]
    grad = grad_ref[...].astype(f32)
    first = jnp.dot(first_mask[...], slots, preferred_element_type=f32)
    second = jnp.dot(second_mask[...], slots, preferred_element_type=f32)
    mixed = frames_ref[...].astype(f32) + gate_columns[:, 0:1] * first
    mixed_ref[...] = (mixed + gate_columns[:, 1:2] * second).astype(bf16)
    sums[:, 0:1] += jnp.sum(first * grad, axis=1, keepdims=True)
    sums[:, 1:2] += jnp.sum(second * grad, axis=1, keepdims=True)

    @pl.when(step == pl.num_programs(0) - 1)
    def _():
        gate_grad_ref[0:1, :] = to_row(sums[:, 0:1])
        gate_grad_ref[1:2, :] = to_row(sums[:, 1:2])


def mix(target, gates, slots, frames, grad, tile=512):
    rows, width = frames.shape
    n = slots.shape[0]
    return pl.pallas_call(
        mix_kernel,
        grid=(width // tile,),
        out_shape=(
            jax.ShapeDtypeStruct((rows, width), bf16),
            jax.ShapeDtypeStruct((2, rows), f32),
        ),
        in_specs=[
            whole((2, rows)),
            whole((2, rows)),
            cols(n, tile),
            cols(rows, tile),
            cols(rows, tile),
        ],
        out_specs=(cols(rows, tile), whole((2, rows))),
        scratch_shapes=[
            pltpu.VMEM((rows, n), bf16),
            pltpu.VMEM((rows, n), bf16),
            pltpu.VMEM((rows, 2), f32),
            pltpu.VMEM((rows, 2), f32),
        ],
        cost_estimate=cost(4 * n * rows * width, 2 * (n + 3 * rows) * width),
        name="mix",
    )(target, gates, slots, frames, grad)


def head_kernel(low_ref, block_ref, high_ref, taps_ref, head_ref, logits_ref, padded):
    rows, width = block_ref.shape
    taps = taps_ref.shape[0]
    fill_padded(padded, low_ref[...], block_ref[...], high_ref[...])
    summed = jnp.zeros(block_ref.shape, f32)
    for offset in range(taps):
        start = 8 - taps // 2 + offset
        summed = summed + taps_ref[offset : offset + 1, :] * padded[start : start + rows, :]
    logits_ref[...] += lax.dot_general(
        head_ref[...], summed.astype(bf16), (((1,), (1,)), ((), ())), preferred_element_type=f32
    )


def head_step(low_ref, block_ref, high_ref, taps_ref, head_ref, logits_ref, padded, total):
    step = pl.program_id(0)

    @pl.when(step == 0)
    def _():
        total[...] = jnp.zeros_like(total)

    head_kernel(low_ref, block_ref, high_ref, taps_ref, head_ref, total, padded)

    @pl.when(step == pl.num_programs(0) - 1)
    def _():
        logits_ref[...] = total[...].astype(bf16)


def head(low, block, high, taps, head_t, tile=512):
    rows, width = block.shape
    margin = low.shape[0]
    classes = head_t.shape[0]
    return pl.pallas_call(
        head_step,
        grid=(width // tile,),
        out_shape=jax.ShapeDtypeStruct((classes, rows), bf16),
        in_specs=[
            cols(margin, tile),
            cols(rows, tile),
            cols(margin, tile),
            cols(taps.shape[0], tile),
            cols(classes, tile),
        ],
        out_specs=whole((classes, rows)),
        scratch_shapes=[
            pltpu.VMEM((rows + 16, tile), f32),
            pltpu.VMEM((classes, rows), f32),
        ],
        cost_estimate=cost(2 * classes * rows * width, 2 * (classes + rows) * width),
        name="head",
    )(low, block, high, taps, head_t)


def finish_kernel(
    target_ref, gates_ref, slots_ref, grad_ref, out_ref, first_mask, second_mask, gate_columns
):
    @pl.when(pl.program_id(0) == 0)
    def _():
        target = target_ref[...]
        gates = gates_ref[...]
        first_mask[...] = pick_mask(target[0:1, :], first_mask.shape[1])
        second_mask[...] = pick_mask(target[1:2, :], second_mask.shape[1])
        gate_columns[:, 0:1] = to_column(gates[0:1, :])
        gate_columns[:, 1:2] = to_column(gates[1:2, :])

    slots = slots_ref[...]
    first = jnp.dot(first_mask[...], slots, preferred_element_type=f32)
    second = jnp.dot(second_mask[...], slots, preferred_element_type=f32)
    total = grad_ref[...].astype(f32) + gate_columns[:, 0:1] * first
    out_ref[...] = (total + gate_columns[:, 1:2] * second).astype(bf16)


def finish(target, gates, slots, grad, tile=512):
    rows, width = grad.shape
    n = slots.shape[0]
    return pl.pallas_call(
        finish_kernel,
        grid=(width // tile,),
        out_shape=jax.ShapeDtypeStruct((rows, width), bf16),
        in_specs=[whole((2, rows)), whole((2, rows)), cols(n, tile), cols(rows, tile)],
        out_specs=cols(rows, tile),
        scratch_shapes=[
            pltpu.VMEM((rows, n), bf16),
            pltpu.VMEM((rows, n), bf16),
            pltpu.VMEM((rows, 2), f32),
        ],
        cost_estimate=cost(4 * n * rows * width, 2 * (n + 2 * rows) * width),
        name="finish",
    )(target, gates, slots, grad)


def edges(block, width):
    axes = ("seq", "expert")
    count = lax.axis_size(axes)
    forward = [(i, i + 1) for i in range(count - 1)]
    backward = [(target, source) for source, target in forward]
    low = lax.ppermute(block[block.shape[0] - width :], axes, forward)
    high = lax.ppermute(block[:width], axes, backward)
    return low, high


def exchange(slots, owners):
    blocks = slots.reshape(owners, -1, slots.shape[1])
    blocks = lax.all_to_all(blocks, "expert", split_axis=0, concat_axis=0, tiled=True)
    return blocks.reshape(slots.shape)


def body(
    frames, expert_ids, gate_weights, up_weight, down_weight, smooth_taps, head_weight, logit_grad
):
    owners = lax.axis_size("expert")
    local_rows = frames.shape[0]
    capacity = 4 * local_rows // owners
    slots = owners * capacity
    margin = smooth_taps.shape[0] // 2
    up_one = up_weight[0]
    down_one = down_weight[0]
    gates = gate_weights.T
    head_t = head_weight.T

    send_x, target = dispatch(expert_ids.T, frames, owners, capacity)
    got_x = exchange(send_x, owners)

    smooth_grad = jnp.einsum(
        "fc,dc->fd", logit_grad, head_weight, preferred_element_type=f32
    ).astype(bf16)
    smooth_grad = lax.optimization_barrier(smooth_grad)
    low, high = edges(smooth_grad, margin)
    mixed_grad, send_g = grad_dispatch(target, low, smooth_grad, high, smooth_taps, slots)
    got_g = exchange(send_g, owners)

    pre = jnp.dot(got_x, up_one, preferred_element_type=f32)
    hidden = gelu_value(pre).astype(bf16)
    outputs = jnp.dot(hidden, down_one, preferred_element_type=f32).astype(bf16)
    out_slots = exchange(outputs, owners)

    back_hidden = jnp.einsum("rd,hd->rh", got_g, down_one, preferred_element_type=f32)
    pre_grad = (back_hidden * gelu_slope(pre)).astype(bf16)
    parts = jnp.einsum("rh,dh->rd", pre_grad, up_one, preferred_element_type=f32).astype(bf16)
    part_slots = exchange(parts, owners)

    mixed, gate_grad = mix(target, gates, out_slots, frames, mixed_grad)
    low, high = edges(mixed, margin)
    logits = head(low, mixed, high, smooth_taps, head_t)
    frame_grad = finish(target, gates, part_slots, mixed_grad)
    return (logits.T, frame_grad, gate_grad.T)


def solution(mesh):
    placed = (
        P(("seq", "expert"), None),
        P(("seq", "expert"), None),
        P(("seq", "expert"), None),
        P("expert", None, None),
        P("expert", None, None),
        P(),
        P(),
        P(("seq", "expert"), None),
    )
    return jax.shard_map(
        body,
        mesh=mesh,
        in_specs=placed,
        out_specs=(
            P(("seq", "expert"), None),
            P(("seq", "expert"), None),
            P(("seq", "expert"), None),
        ),
        check_vma=False,
    )
```

```python
import functools

import jax
import jax.numpy as jnp
from jax import lax
from jax.experimental import pallas as pl
from jax.experimental.pallas import tpu as pltpu
from jax.sharding import PartitionSpec as P


slope_coef = 0.7978845608028654
cubic_coef = 0.044715
bf16 = jnp.bfloat16
f32 = jnp.float32
i32 = jnp.int32


def gelu_value(inputs):
    return (
        0.5
        * inputs
        * (1.0 + jnp.tanh(slope_coef * (inputs + cubic_coef * inputs * inputs * inputs)))
    )


def gelu_slope(inputs):
    inner = jnp.tanh(slope_coef * (inputs + cubic_coef * inputs * inputs * inputs))
    return 0.5 * (1.0 + inner) + 0.5 * inputs * (1.0 - inner * inner) * slope_coef * (
        1.0 + 3.0 * cubic_coef * inputs * inputs
    )


def cost(flops, moved):
    return pl.CostEstimate(flops=flops, bytes_accessed=moved, transcendentals=0)


def params(mib):
    return pltpu.CompilerParams(vmem_limit_bytes=mib << 20)


def resident(count):
    return [pl.BlockSpec(memory_space=pltpu.VMEM)] * count


def tiles(width, tile=512):
    return [slice(start, start + tile) for start in range(0, width, tile)]


def iota(shape, dim):
    return lax.broadcasted_iota(i32, shape, dim)


def to_column(row):
    n = row.shape[1]
    diagonal = iota((n, n), 0) == iota((n, n), 1)
    return jnp.sum(jnp.where(diagonal, row, jnp.zeros_like(row)), axis=1, keepdims=True)


def to_row(column):
    n = column.shape[0]
    diagonal = iota((n, n), 0) == iota((n, n), 1)
    return jnp.sum(jnp.where(diagonal, column, jnp.zeros_like(column)), axis=0, keepdims=True)


def send_mask(target, slots):
    rows = iota((slots, target.shape[1]), 0)
    hit = (rows == target[0:1, :]) | (rows == target[1:2, :])
    return jnp.where(hit, 1.0, 0.0).astype(bf16)


def pick_mask(target_row, slots):
    column = to_column(target_row)
    return jnp.where(iota((column.shape[0], slots), 1) == column, 1.0, 0.0).astype(bf16)


def convolve(padded, taps_ref, part, rows, first_row, step):
    taps = taps_ref.shape[0]
    summed = jnp.zeros((rows, part.stop - part.start), f32)
    for offset in range(taps):
        start = first_row + (offset if step == 1 else taps - 1 - offset)
        summed = summed + taps_ref[offset : offset + 1, part] * padded[start : start + rows, part]
    return summed


def inner_rows(block_ref, padded):
    rows, width = block_ref.shape
    padded[0:8, :] = jnp.zeros((8, width), f32)
    padded[8 : 8 + rows, :] = block_ref[...].astype(f32)
    padded[8 + rows : 16 + rows, :] = jnp.zeros((8, width), f32)


def outer_rows(low_ref, edge_ref, high_ref, padded):
    margin = low_ref.shape[0]
    padded[8 - margin : 8, :] = low_ref[...].astype(f32)
    padded[8:24, :] = edge_ref[...].astype(f32)
    padded[24 : 24 + margin, :] = high_ref[...].astype(f32)


def at_ends(low, high, rows):
    margin, n = low.shape
    gap = jnp.zeros((8 - margin, n), f32)
    middle = jnp.zeros((rows - 16, n), f32)
    return jnp.concatenate([low, gap, middle, gap, high], axis=0)


def iota(shape, dim):
    return lax.broadcasted_iota(i32, shape, dim)


def to_column(row):
    n = row.shape[1]
    diagonal = iota((n, n), 0) == iota((n, n), 1)
    return jnp.sum(jnp.where(diagonal, row, jnp.zeros_like(row)), axis=1, keepdims=True)


def to_row(column):
    n = column.shape[0]
    diagonal = iota((n, n), 0) == iota((n, n), 1)
    return jnp.sum(jnp.where(diagonal, column, jnp.zeros_like(column)), axis=0, keepdims=True)


def send_mask(target, slots):
    rows = iota((slots, target.shape[1]), 0)
    hit = (rows == target[0:1, :]) | (rows == target[1:2, :])
    return jnp.where(hit, 1.0, 0.0).astype(bf16)


def pick_mask(target_row, slots):
    column = to_column(target_row)
    return jnp.where(iota((column.shape[0], slots), 1) == column, 1.0, 0.0).astype(bf16)


def slot_targets(ids, owners, capacity):
    count = ids.shape[1]
    first, second = ids[0:1, :], ids[1:2, :]
    experts = iota((owners, count), 0)
    first_hot = jnp.where(experts == first, 1.0, 0.0)
    second_hot = jnp.where(experts == second, 1.0, 0.0)
    before = jnp.where(iota((count, count), 0) < iota((count, count), 1), 1.0, 0.0).astype(bf16)
    first_seen = jnp.dot(first_hot.astype(bf16), before, preferred_element_type=f32)
    second_seen = jnp.dot(second_hot.astype(bf16), before, preferred_element_type=f32)
    second_seen = second_seen + jnp.sum(first_hot, axis=1, keepdims=True)
    first_rank = jnp.sum(first_seen * first_hot, axis=0, keepdims=True).astype(i32)
    second_rank = jnp.sum(second_seen * second_hot, axis=0, keepdims=True).astype(i32)
    return jnp.concatenate(
        [first * capacity + first_rank, second * capacity + second_rank], axis=0
    )


def dispatch_kernel(owners, capacity, ids_ref, frames_ref, send_ref, target_ref):
    target = slot_targets(ids_ref[...], owners, capacity)
    target_ref[...] = target
    mask = send_mask(target, owners * capacity)
    for part in tiles(frames_ref.shape[1]):
        send_ref[:, part] = jnp.dot(
            mask, frames_ref[:, part], preferred_element_type=f32
        ).astype(bf16)


def dispatch(ids, frames, owners, capacity):
    rows, width = frames.shape
    slots = owners * capacity
    return pl.pallas_call(
        functools.partial(dispatch_kernel, owners, capacity),
        out_shape=(
            jax.ShapeDtypeStruct((slots, width), bf16),
            jax.ShapeDtypeStruct((2, rows), i32),
        ),
        in_specs=resident(2),
        out_specs=tuple(resident(2)),
        cost_estimate=cost(2 * slots * rows * width, 2 * (slots + rows) * width),
        compiler_params=params(60),
        name="dispatch",
    )(ids, frames)


def keep_edges(block_ref, edge_ref):
    rows = block_ref.shape[0]
    edge_ref[0:8, :] = block_ref[0:8, :]
    edge_ref[8:16, :] = block_ref[rows - 8 : rows, :]


def grad_inner_kernel(block_ref, taps_ref, inner_ref, edge_ref, padded):
    rows, width = block_ref.shape
    inner_rows(block_ref, padded)
    keep_edges(block_ref, edge_ref)
    start = 8 - taps_ref.shape[0] // 2
    for part in tiles(width):
        inner_ref[:, part] = convolve(padded, taps_ref, part, rows, start, -1).astype(bf16)


def grad_inner(block, taps):
    rows, width = block.shape
    return pl.pallas_call(
        grad_inner_kernel,
        out_shape=(
            jax.ShapeDtypeStruct((rows, width), bf16),
            jax.ShapeDtypeStruct((16, width), bf16),
        ),
        in_specs=resident(2),
        out_specs=tuple(resident(2)),
        scratch_shapes=[pltpu.VMEM((rows + 16, width), f32)],
        cost_estimate=cost(18 * rows * width, 4 * rows * width),
        compiler_params=params(8),
        name="grad_inner",
    )(block, taps)


def grad_kernel(
    target_ref, low_ref, edge_ref, high_ref, inner_ref, taps_ref, grad_ref, send_ref, padded
):
    rows, width = inner_ref.shape
    margin = low_ref.shape[0]
    outer_rows(low_ref, edge_ref, high_ref, padded)
    mask = send_mask(target_ref[...], send_ref.shape[0])
    frame = iota((rows, 1), 0)
    outer = (frame < margin) | (frame >= rows - margin)
    for part in tiles(width):
        first = convolve(padded, taps_ref, part, margin, 8 - margin, -1)
        last = convolve(padded, taps_ref, part, margin, 24 - 2 * margin, -1)
        ends = at_ends(first, last, rows)
        grad = jnp.where(outer, ends, inner_ref[:, part].astype(f32)).astype(bf16)
        grad_ref[:, part] = grad
        send_ref[:, part] = jnp.dot(mask, grad, preferred_element_type=f32).astype(bf16)


def grad_dispatch(target, low, edge, high, inner, taps, slots):
    rows, width = inner.shape
    return pl.pallas_call(
        grad_kernel,
        out_shape=(
            jax.ShapeDtypeStruct((rows, width), bf16),
            jax.ShapeDtypeStruct((slots, width), bf16),
        ),
        in_specs=resident(6),
        out_specs=tuple(resident(2)),
        scratch_shapes=[pltpu.VMEM((32, width), f32)],
        cost_estimate=cost(2 * slots * rows * width, 2 * (slots + 2 * rows) * width),
        compiler_params=params(8),
        name="grad_dispatch",
    )(target, low, edge, high, inner, taps)


def mix_kernel(target_ref, gates_ref, slots_ref, frames_ref, grad_ref, mixed_ref, gate_grad_ref):
    rows, width = frames_ref.shape
    slots = slots_ref.shape[0]
    masks = [pick_mask(target_ref[k : k + 1, :], slots) for k in range(2)]
    gates = [to_column(gates_ref[k : k + 1, :]) for k in range(2)]
    sums = [jnp.zeros((rows, 1), f32) for _ in range(2)]
    for part in tiles(width):
        grad = grad_ref[:, part].astype(f32)
        mixed = frames_ref[:, part].astype(f32)
        for k in range(2):
            picked = jnp.dot(masks[k], slots_ref[:, part], preferred_element_type=f32)
            mixed = mixed + gates[k] * picked
            sums[k] = sums[k] + jnp.sum(picked * grad, axis=1, keepdims=True)
        mixed_ref[:, part] = mixed.astype(bf16)
    for k in range(2):
        gate_grad_ref[k : k + 1, :] = to_row(sums[k])


def mix(target, gates, slots, frames, grad):
    rows, width = frames.shape
    n = slots.shape[0]
    return pl.pallas_call(
        mix_kernel,
        out_shape=(
            jax.ShapeDtypeStruct((rows, width), bf16),
            jax.ShapeDtypeStruct((2, rows), f32),
        ),
        in_specs=resident(5),
        out_specs=tuple(resident(2)),
        cost_estimate=cost(4 * n * rows * width, 2 * (n + 3 * rows) * width),
        compiler_params=params(60),
        name="mix",
    )(target, gates, slots, frames, grad)


def classes_of(head_ref, part, smooth):
    return lax.dot_general(
        head_ref[:, part], smooth, (((1,), (1,)), ((), ())), preferred_element_type=f32
    )


def head_inner_kernel(block_ref, taps_ref, head_ref, logits_ref, edge_ref, padded):
    rows, width = block_ref.shape
    inner_rows(block_ref, padded)
    keep_edges(block_ref, edge_ref)
    total = jnp.zeros(logits_ref.shape, f32)
    start = 8 - taps_ref.shape[0] // 2
    for part in tiles(width):
        smooth = convolve(padded, taps_ref, part, rows, start, 1).astype(bf16)
        total = total + classes_of(head_ref, part, smooth)
    logits_ref[...] = total.astype(bf16)


def head_inner(block, taps, head_t):
    rows, width = block.shape
    classes = head_t.shape[0]
    return pl.pallas_call(
        head_inner_kernel,
        out_shape=(
            jax.ShapeDtypeStruct((classes, rows), bf16),
            jax.ShapeDtypeStruct((16, width), bf16),
        ),
        in_specs=resident(3),
        out_specs=tuple(resident(2)),
        scratch_shapes=[pltpu.VMEM((rows + 16, width), f32)],
        cost_estimate=cost(2 * classes * rows * width, 2 * (classes + rows) * width),
        compiler_params=params(8),
        name="head_inner",
    )(block, taps, head_t)


def head_outer_kernel(
    low_ref, edge_ref, high_ref, taps_ref, head_ref, inner_ref, logits_ref, padded
):
    rows = inner_ref.shape[1]
    width = edge_ref.shape[1]
    margin = low_ref.shape[0]
    outer_rows(low_ref, edge_ref, high_ref, padded)
    total = jnp.zeros(inner_ref.shape, f32)
    for part in tiles(width):
        first = convolve(padded, taps_ref, part, margin, 8 - margin, 1)
        last = convolve(padded, taps_ref, part, margin, 24 - 2 * margin, 1)
        total = total + classes_of(head_ref, part, at_ends(first, last, rows).astype(bf16))
    frame = iota((1, rows), 1)
    outer = (frame < margin) | (frame >= rows - margin)
    logits_ref[...] = jnp.where(outer, total, inner_ref[...].astype(f32)).astype(bf16)


def head_outer(low, edge, high, taps, head_t, inner):
    classes, rows = inner.shape
    width = edge.shape[1]
    return pl.pallas_call(
        head_outer_kernel,
        out_shape=jax.ShapeDtypeStruct((classes, rows), bf16),
        in_specs=resident(6),
        out_specs=resident(1)[0],
        scratch_shapes=[pltpu.VMEM((32, width), f32)],
        cost_estimate=cost(2 * classes * rows * width, 2 * (classes + rows) * width),
        compiler_params=params(8),
        name="head_outer",
    )(low, edge, high, taps, head_t, inner)


def finish_kernel(target_ref, gates_ref, slots_ref, grad_ref, out_ref):
    slots = slots_ref.shape[0]
    masks = [pick_mask(target_ref[k : k + 1, :], slots) for k in range(2)]
    gates = [to_column(gates_ref[k : k + 1, :]) for k in range(2)]
    for part in tiles(grad_ref.shape[1]):
        total = grad_ref[:, part].astype(f32)
        for k in range(2):
            total = total + gates[k] * jnp.dot(
                masks[k], slots_ref[:, part], preferred_element_type=f32
            )
        out_ref[:, part] = total.astype(bf16)


def finish(target, gates, slots, grad):
    rows, width = grad.shape
    n = slots.shape[0]
    return pl.pallas_call(
        finish_kernel,
        out_shape=jax.ShapeDtypeStruct((rows, width), bf16),
        in_specs=resident(4),
        out_specs=resident(1)[0],
        cost_estimate=cost(4 * n * rows * width, 2 * (n + 2 * rows) * width),
        compiler_params=params(8),
        name="finish",
    )(target, gates, slots, grad)


def keep_kernel(gates_ref, out_ref):
    out_ref[...] = gates_ref[...]


def keep(gates):
    return pl.pallas_call(
        keep_kernel,
        out_shape=jax.ShapeDtypeStruct(gates.shape, gates.dtype),
        in_specs=resident(1),
        out_specs=resident(1)[0],
        compiler_params=pltpu.CompilerParams(vmem_limit_bytes=67043328 - 1000000),
        name="keep",
    )(gates)


def edges(block, width):
    axes = ("seq", "expert")
    count = lax.axis_size(axes)
    forward = [(i, i + 1) for i in range(count - 1)]
    backward = [(target, source) for source, target in forward]
    low = lax.ppermute(block[block.shape[0] - width :], axes, forward)
    high = lax.ppermute(block[:width], axes, backward)
    return low, high


def exchange(slots, owners):
    blocks = slots.reshape(owners, -1, slots.shape[1])
    blocks = lax.all_to_all(blocks, "expert", split_axis=0, concat_axis=0, tiled=True)
    return blocks.reshape(slots.shape)


def layer(
    frames, expert_ids, gate_weights, up_weight, down_weight, smooth_taps, head_weight, logit_grad
):
    owners = lax.axis_size("expert")
    local_rows = frames.shape[0]
    capacity = 4 * local_rows // owners
    slots = owners * capacity
    margin = smooth_taps.shape[0] // 2
    up_one = up_weight[0]
    down_one = down_weight[0]
    gates = gate_weights.T
    head_t = head_weight.T

    send_x, target = dispatch(expert_ids.T, frames, owners, capacity)
    got_x = exchange(send_x, owners)

    smooth_grad = jnp.einsum(
        "fc,dc->fd", logit_grad, head_weight, preferred_element_type=f32
    ).astype(bf16)
    smooth_grad = lax.optimization_barrier(smooth_grad)
    low, high = edges(smooth_grad, margin)
    inner_grad, edge = grad_inner(smooth_grad, smooth_taps)
    mixed_grad, send_g = grad_dispatch(target, low, edge, high, inner_grad, smooth_taps, slots)
    got_g = exchange(send_g, owners)

    pre = jnp.dot(got_x, up_one, preferred_element_type=f32)
    hidden = gelu_value(pre).astype(bf16)
    outputs = jnp.dot(hidden, down_one, preferred_element_type=f32).astype(bf16)
    out_slots = exchange(outputs, owners)
    mix_gates = keep(gates)

    back_hidden = jnp.einsum("rd,hd->rh", got_g, down_one, preferred_element_type=f32)
    pre_grad = (back_hidden * gelu_slope(pre)).astype(bf16)
    parts = jnp.einsum("rh,dh->rd", pre_grad, up_one, preferred_element_type=f32).astype(bf16)
    part_slots = exchange(parts, owners)

    mixed, gate_grad = mix(target, mix_gates, out_slots, frames, mixed_grad)
    low, high = edges(mixed, margin)
    inner_logits, edge = head_inner(mixed, smooth_taps, head_t)
    logits = head_outer(low, edge, high, smooth_taps, head_t, inner_logits)
    frame_grad = finish(target, gates, part_slots, mixed_grad)
    return (logits.T, frame_grad, gate_grad.T)


def solution(mesh):
    placed = (
        P(("seq", "expert"), None),
        P(("seq", "expert"), None),
        P(("seq", "expert"), None),
        P("expert", None, None),
        P("expert", None, None),
        P(),
        P(),
        P(("seq", "expert"), None),
    )
    return jax.shard_map(
        layer,
        mesh=mesh,
        in_specs=placed,
        out_specs=(
            P(("seq", "expert"), None),
            P(("seq", "expert"), None),
            P(("seq", "expert"), None),
        ),
        check_vma=False,
    )
```

```python
import functools

import jax
import jax.numpy as jnp
from jax import lax
from jax.experimental import pallas as pl
from jax.experimental.pallas import tpu as pltpu
from jax.sharding import PartitionSpec as P


slope_coef = 0.7978845608028654
cubic_coef = 0.044715
bf16 = jnp.bfloat16
f32 = jnp.float32
i32 = jnp.int32


def gelu_value(inputs):
    return (
        0.5
        * inputs
        * (1.0 + jnp.tanh(slope_coef * (inputs + cubic_coef * inputs * inputs * inputs)))
    )


def gelu_slope(inputs):
    inner = jnp.tanh(slope_coef * (inputs + cubic_coef * inputs * inputs * inputs))
    return 0.5 * (1.0 + inner) + 0.5 * inputs * (1.0 - inner * inner) * slope_coef * (
        1.0 + 3.0 * cubic_coef * inputs * inputs
    )


def cost(flops, moved):
    return pl.CostEstimate(flops=flops, bytes_accessed=moved, transcendentals=0)


def params(mib):
    return pltpu.CompilerParams(vmem_limit_bytes=mib << 20)


def resident(count):
    return [pl.BlockSpec(memory_space=pltpu.VMEM)] * count


def tiles(width, tile=256):
    return [slice(start, start + tile) for start in range(0, width, tile)]


def iota(shape, dim):
    return lax.broadcasted_iota(i32, shape, dim)


def to_column(row):
    n = row.shape[1]
    diagonal = iota((n, n), 0) == iota((n, n), 1)
    return jnp.sum(jnp.where(diagonal, row, jnp.zeros_like(row)), axis=1, keepdims=True)


def to_row(column):
    n = column.shape[0]
    diagonal = iota((n, n), 0) == iota((n, n), 1)
    return jnp.sum(jnp.where(diagonal, column, jnp.zeros_like(column)), axis=0, keepdims=True)


def send_mask(target, slots):
    rows = iota((slots, target.shape[1]), 0)
    hit = (rows == target[0:1, :]) | (rows == target[1:2, :])
    return jnp.where(hit, 1.0, 0.0).astype(bf16)


def pick_mask(target_row, slots):
    column = to_column(target_row)
    return jnp.where(iota((column.shape[0], slots), 1) == column, 1.0, 0.0).astype(bf16)


def convolve(padded, taps_ref, part, rows, first_row, step):
    taps = taps_ref.shape[0]
    summed = jnp.zeros((rows, part.stop - part.start), f32)
    for offset in range(taps):
        start = first_row + (offset if step == 1 else taps - 1 - offset)
        summed = summed + taps_ref[offset : offset + 1, part] * padded[start : start + rows, part]
    return summed


def inner_rows(block_ref, padded):
    rows, width = block_ref.shape
    padded[0:8, :] = jnp.zeros((8, width), f32)
    padded[8 : 8 + rows, :] = block_ref[...].astype(f32)
    padded[8 + rows : 16 + rows, :] = jnp.zeros((8, width), f32)


def outer_rows(low_ref, edge_ref, high_ref, padded):
    margin = low_ref.shape[0]
    padded[8 - margin : 8, :] = low_ref[...].astype(f32)
    padded[8:24, :] = edge_ref[...].astype(f32)
    padded[24 : 24 + margin, :] = high_ref[...].astype(f32)


def at_ends(low, high, rows):
    margin, n = low.shape
    gap = jnp.zeros((8 - margin, n), f32)
    middle = jnp.zeros((rows - 16, n), f32)
    return jnp.concatenate([low, gap, middle, gap, high], axis=0)


def iota(shape, dim):
    return lax.broadcasted_iota(i32, shape, dim)


def to_column(row):
    n = row.shape[1]
    diagonal = iota((n, n), 0) == iota((n, n), 1)
    return jnp.sum(jnp.where(diagonal, row, jnp.zeros_like(row)), axis=1, keepdims=True)


def to_row(column):
    n = column.shape[0]
    diagonal = iota((n, n), 0) == iota((n, n), 1)
    return jnp.sum(jnp.where(diagonal, column, jnp.zeros_like(column)), axis=0, keepdims=True)


def send_mask(target, slots):
    rows = iota((slots, target.shape[1]), 0)
    hit = (rows == target[0:1, :]) | (rows == target[1:2, :])
    return jnp.where(hit, 1.0, 0.0).astype(bf16)


def pick_mask(target_row, slots):
    column = to_column(target_row)
    return jnp.where(iota((column.shape[0], slots), 1) == column, 1.0, 0.0).astype(bf16)


def slot_targets(ids, owners, capacity):
    count = ids.shape[1]
    first, second = ids[0:1, :], ids[1:2, :]
    experts = iota((owners, count), 0)
    first_hot = jnp.where(experts == first, 1.0, 0.0)
    second_hot = jnp.where(experts == second, 1.0, 0.0)
    before = jnp.where(iota((count, count), 0) < iota((count, count), 1), 1.0, 0.0).astype(bf16)
    first_seen = jnp.dot(first_hot.astype(bf16), before, preferred_element_type=f32)
    second_seen = jnp.dot(second_hot.astype(bf16), before, preferred_element_type=f32)
    second_seen = second_seen + jnp.sum(first_hot, axis=1, keepdims=True)
    first_rank = jnp.sum(first_seen * first_hot, axis=0, keepdims=True).astype(i32)
    second_rank = jnp.sum(second_seen * second_hot, axis=0, keepdims=True).astype(i32)
    return jnp.concatenate(
        [first * capacity + first_rank, second * capacity + second_rank], axis=0
    )


def dispatch_kernel(owners, capacity, ids_ref, frames_ref, send_ref, target_ref):
    target = slot_targets(ids_ref[...], owners, capacity)
    target_ref[...] = target
    mask = send_mask(target, owners * capacity)
    for part in tiles(frames_ref.shape[1]):
        send_ref[:, part] = jnp.dot(
            mask, frames_ref[:, part], preferred_element_type=f32
        ).astype(bf16)


def dispatch(ids, frames, owners, capacity):
    rows, width = frames.shape
    slots = owners * capacity
    return pl.pallas_call(
        functools.partial(dispatch_kernel, owners, capacity),
        out_shape=(
            jax.ShapeDtypeStruct((slots, width), bf16),
            jax.ShapeDtypeStruct((2, rows), i32),
        ),
        in_specs=resident(2),
        out_specs=tuple(resident(2)),
        cost_estimate=cost(2 * slots * rows * width, 2 * (slots + rows) * width),
        compiler_params=params(60),
        name="dispatch",
    )(ids, frames)


def keep_edges(block_ref, edge_ref):
    rows = block_ref.shape[0]
    edge_ref[0:8, :] = block_ref[0:8, :]
    edge_ref[8:16, :] = block_ref[rows - 8 : rows, :]


def grad_inner_kernel(block_ref, taps_ref, inner_ref, edge_ref, padded):
    rows, width = block_ref.shape
    inner_rows(block_ref, padded)
    keep_edges(block_ref, edge_ref)
    start = 8 - taps_ref.shape[0] // 2
    for part in tiles(width):
        inner_ref[:, part] = convolve(padded, taps_ref, part, rows, start, -1).astype(bf16)


def grad_inner(block, taps):
    rows, width = block.shape
    return pl.pallas_call(
        grad_inner_kernel,
        out_shape=(
            jax.ShapeDtypeStruct((rows, width), bf16),
            jax.ShapeDtypeStruct((16, width), bf16),
        ),
        in_specs=resident(2),
        out_specs=tuple(resident(2)),
        scratch_shapes=[pltpu.VMEM((rows + 16, width), f32)],
        cost_estimate=cost(18 * rows * width, 4 * rows * width),
        compiler_params=params(8),
        name="grad_inner",
    )(block, taps)


def grad_kernel(
    target_ref, low_ref, edge_ref, high_ref, inner_ref, taps_ref, grad_ref, send_ref, padded
):
    rows, width = inner_ref.shape
    margin = low_ref.shape[0]
    outer_rows(low_ref, edge_ref, high_ref, padded)
    mask = send_mask(target_ref[...], send_ref.shape[0])
    frame = iota((rows, 1), 0)
    outer = (frame < margin) | (frame >= rows - margin)
    for part in tiles(width):
        first = convolve(padded, taps_ref, part, margin, 8 - margin, -1)
        last = convolve(padded, taps_ref, part, margin, 24 - 2 * margin, -1)
        ends = at_ends(first, last, rows)
        grad = jnp.where(outer, ends, inner_ref[:, part].astype(f32)).astype(bf16)
        grad_ref[:, part] = grad
        send_ref[:, part] = jnp.dot(mask, grad, preferred_element_type=f32).astype(bf16)


def grad_dispatch(target, low, edge, high, inner, taps, slots):
    rows, width = inner.shape
    return pl.pallas_call(
        grad_kernel,
        out_shape=(
            jax.ShapeDtypeStruct((rows, width), bf16),
            jax.ShapeDtypeStruct((slots, width), bf16),
        ),
        in_specs=resident(6),
        out_specs=tuple(resident(2)),
        scratch_shapes=[pltpu.VMEM((32, width), f32)],
        cost_estimate=cost(2 * slots * rows * width, 2 * (slots + 2 * rows) * width),
        compiler_params=params(8),
        name="grad_dispatch",
    )(target, low, edge, high, inner, taps)


def mix_kernel(target_ref, gates_ref, slots_ref, frames_ref, grad_ref, mixed_ref, gate_grad_ref):
    rows, width = frames_ref.shape
    slots = slots_ref.shape[0]
    masks = [pick_mask(target_ref[k : k + 1, :], slots) for k in range(2)]
    gates = [to_column(gates_ref[k : k + 1, :]) for k in range(2)]
    sums = [jnp.zeros((rows, 1), f32) for _ in range(2)]
    for part in tiles(width):
        grad = grad_ref[:, part].astype(f32)
        mixed = frames_ref[:, part].astype(f32)
        for k in range(2):
            picked = jnp.dot(masks[k], slots_ref[:, part], preferred_element_type=f32)
            mixed = mixed + gates[k] * picked
            sums[k] = sums[k] + jnp.sum(picked * grad, axis=1, keepdims=True)
        mixed_ref[:, part] = mixed.astype(bf16)
    for k in range(2):
        gate_grad_ref[k : k + 1, :] = to_row(sums[k])


def mix(target, gates, slots, frames, grad):
    rows, width = frames.shape
    n = slots.shape[0]
    return pl.pallas_call(
        mix_kernel,
        out_shape=(
            jax.ShapeDtypeStruct((rows, width), bf16),
            jax.ShapeDtypeStruct((2, rows), f32),
        ),
        in_specs=resident(5),
        out_specs=tuple(resident(2)),
        cost_estimate=cost(4 * n * rows * width, 2 * (n + 3 * rows) * width),
        compiler_params=params(8),
        name="mix",
    )(target, gates, slots, frames, grad)


def classes_of(head_ref, part, smooth):
    return lax.dot_general(
        head_ref[:, part], smooth, (((1,), (1,)), ((), ())), preferred_element_type=f32
    )


def head_inner_kernel(block_ref, taps_ref, head_ref, logits_ref, edge_ref, near_ref, padded):
    rows, width = block_ref.shape
    near_ref[...] = head_ref[...]
    inner_rows(block_ref, padded)
    keep_edges(block_ref, edge_ref)
    total = jnp.zeros(logits_ref.shape, f32)
    start = 8 - taps_ref.shape[0] // 2
    for part in tiles(width):
        smooth = convolve(padded, taps_ref, part, rows, start, 1).astype(bf16)
        total = total + classes_of(head_ref, part, smooth)
    logits_ref[...] = total.astype(bf16)


def head_inner(block, taps, head_t):
    rows, width = block.shape
    classes = head_t.shape[0]
    return pl.pallas_call(
        head_inner_kernel,
        out_shape=(
            jax.ShapeDtypeStruct((classes, rows), bf16),
            jax.ShapeDtypeStruct((16, width), bf16),
            jax.ShapeDtypeStruct((classes, width), bf16),
        ),
        in_specs=resident(3),
        out_specs=tuple(resident(3)),
        scratch_shapes=[pltpu.VMEM((rows + 16, width), f32)],
        cost_estimate=cost(2 * classes * rows * width, 2 * (classes + rows) * width),
        compiler_params=params(8),
        name="head_inner",
    )(block, taps, head_t)


def head_outer_kernel(
    low_ref, edge_ref, high_ref, taps_ref, head_ref, inner_ref, logits_ref, padded
):
    rows = inner_ref.shape[1]
    width = edge_ref.shape[1]
    margin = low_ref.shape[0]
    outer_rows(low_ref, edge_ref, high_ref, padded)
    total = jnp.zeros(inner_ref.shape, f32)
    for part in tiles(width):
        first = convolve(padded, taps_ref, part, margin, 8 - margin, 1)
        last = convolve(padded, taps_ref, part, margin, 24 - 2 * margin, 1)
        total = total + classes_of(head_ref, part, at_ends(first, last, rows).astype(bf16))
    frame = iota((1, rows), 1)
    outer = (frame < margin) | (frame >= rows - margin)
    logits_ref[...] = jnp.where(outer, total, inner_ref[...].astype(f32)).astype(bf16)


def head_outer(low, edge, high, taps, head_t, inner):
    classes, rows = inner.shape
    width = edge.shape[1]
    return pl.pallas_call(
        head_outer_kernel,
        out_shape=jax.ShapeDtypeStruct((classes, rows), bf16),
        in_specs=resident(6),
        out_specs=resident(1)[0],
        scratch_shapes=[pltpu.VMEM((32, width), f32)],
        cost_estimate=cost(2 * classes * rows * width, 2 * (classes + rows) * width),
        compiler_params=params(8),
        name="head_outer",
    )(low, edge, high, taps, head_t, inner)


def finish_kernel(target_ref, gates_ref, slots_ref, grad_ref, out_ref):
    slots = slots_ref.shape[0]
    masks = [pick_mask(target_ref[k : k + 1, :], slots) for k in range(2)]
    gates = [to_column(gates_ref[k : k + 1, :]) for k in range(2)]
    for part in tiles(grad_ref.shape[1]):
        total = grad_ref[:, part].astype(f32)
        for k in range(2):
            total = total + gates[k] * jnp.dot(
                masks[k], slots_ref[:, part], preferred_element_type=f32
            )
        out_ref[:, part] = total.astype(bf16)


def finish(target, gates, slots, grad):
    rows, width = grad.shape
    n = slots.shape[0]
    return pl.pallas_call(
        finish_kernel,
        out_shape=jax.ShapeDtypeStruct((rows, width), bf16),
        in_specs=resident(4),
        out_specs=resident(1)[0],
        cost_estimate=cost(4 * n * rows * width, 2 * (n + 2 * rows) * width),
        compiler_params=params(8),
        name="finish",
    )(target, gates, slots, grad)


def keep_kernel(gates_ref, out_ref):
    out_ref[...] = gates_ref[...]


def keep(gates):
    return pl.pallas_call(
        keep_kernel,
        out_shape=jax.ShapeDtypeStruct(gates.shape, gates.dtype),
        in_specs=resident(1),
        out_specs=resident(1)[0],
        compiler_params=pltpu.CompilerParams(vmem_limit_bytes=67043328 - 1000000),
        name="keep",
    )(gates)


def edges(block, width):
    axes = ("seq", "expert")
    count = lax.axis_size(axes)
    forward = [(i, i + 1) for i in range(count - 1)]
    backward = [(target, source) for source, target in forward]
    low = lax.ppermute(block[block.shape[0] - width :], axes, forward)
    high = lax.ppermute(block[:width], axes, backward)
    return low, high


def exchange(slots, owners):
    blocks = slots.reshape(owners, -1, slots.shape[1])
    blocks = lax.all_to_all(blocks, "expert", split_axis=0, concat_axis=0, tiled=True)
    return blocks.reshape(slots.shape)


def layer(
    frames, expert_ids, gate_weights, up_weight, down_weight, smooth_taps, head_weight, logit_grad
):
    owners = lax.axis_size("expert")
    local_rows = frames.shape[0]
    capacity = 4 * local_rows // owners
    slots = owners * capacity
    margin = smooth_taps.shape[0] // 2
    up_one = up_weight[0]
    down_one = down_weight[0]
    gates = gate_weights.T
    head_t = head_weight.T

    send_x, target = dispatch(expert_ids.T, frames, owners, capacity)
    got_x = exchange(send_x, owners)

    smooth_grad = jnp.einsum(
        "fc,dc->fd", logit_grad, head_weight, preferred_element_type=f32
    ).astype(bf16)
    smooth_grad = lax.optimization_barrier(smooth_grad)
    low, high = edges(smooth_grad, margin)
    inner_grad, edge = grad_inner(smooth_grad, smooth_taps)
    mixed_grad, send_g = grad_dispatch(target, low, edge, high, inner_grad, smooth_taps, slots)
    got_g = exchange(send_g, owners)

    pre = jnp.dot(got_x, up_one, preferred_element_type=f32)
    hidden = gelu_value(pre).astype(bf16)
    outputs = jnp.dot(hidden, down_one, preferred_element_type=f32).astype(bf16)
    mix_gates = keep(gates)
    out_slots = exchange(outputs, owners)

    back_hidden = jnp.einsum("rd,hd->rh", got_g, down_one, preferred_element_type=f32)
    pre_grad = (back_hidden * gelu_slope(pre)).astype(bf16)
    parts = jnp.einsum("rh,dh->rd", pre_grad, up_one, preferred_element_type=f32).astype(bf16)
    part_slots = exchange(parts, owners)

    mixed, gate_grad = mix(target, mix_gates, out_slots, frames, mixed_grad)
    low, high = edges(mixed, margin)
    inner_logits, edge, near_head = head_inner(mixed, smooth_taps, head_t)
    logits = head_outer(low, edge, high, smooth_taps, near_head, inner_logits)
    gate_grad = keep(gate_grad)
    frame_grad = finish(target, gates, part_slots, mixed_grad)
    return (logits.T, frame_grad, gate_grad.T)


def solution(mesh):
    placed = (
        P(("seq", "expert"), None),
        P(("seq", "expert"), None),
        P(("seq", "expert"), None),
        P("expert", None, None),
        P("expert", None, None),
        P(),
        P(),
        P(("seq", "expert"), None),
    )
    return jax.shard_map(
        layer,
        mesh=mesh,
        in_specs=placed,
        out_specs=(
            P(("seq", "expert"), None),
            P(("seq", "expert"), None),
            P(("seq", "expert"), None),
        ),
        check_vma=False,
    )
```
